32 devices in a mesh: dp: 8 (over z, y), layer: 4 (over x, core).
Axes of the slice: x: 2, y: 2, z: 4, core: 2. Of those that a mesh axis runs over, the one named last changes fastest.
Arguments:
- acts: bfloat16 [4, 16, 128, 4096], P('layer', 'dp'), may hold values from -60 to 60
- grads: bfloat16 [4, 16, 128, 14336], P('layer', 'dp'), may hold values from -60 to 60
- proj_in: bfloat16 [4, 64, 4096], P('layer'), may hold values from -0.09375 to 0.09375
- proj_out: bfloat16 [4, 64, 14336], P('layer'), may hold values from -0.046875 to 0.046875
- query_grads: bfloat16 [4, 512, 4096], P('layer', 'dp'), may hold values from -6 to 6
Outputs:
- scores: float32 [16, 512], P('dp', 'layer')
The draws below stay inside these ranges and needn't reach their ends.
All inputs are finite; a program needn't handle non-finite values.
Results may differ from the reference program's by a relative error of at most 0.004.
Values may be sent and summed in bfloat16 or wider, within the bound.
No kernel may reach another device: no remote copies, remote signals or barrier semaphores. Data moves between devices by JAX's collectives and lax.ppermute only.
A program may use at most 64 MiB of HBM per device.

```python
import jax
import jax.numpy as jnp
from jax import lax

D = 4096
FF = 14336
RANK = 64
SEQ = 128
LAYERS = 4
TRAIN = 16
QUERIES = 512


def structured(key, width, salt):
    key_base, key_dirs, key_coef, key_scale = jax.random.split(jax.random.fold_in(key, salt), 4)
    shape = (LAYERS, TRAIN, SEQ, width)
    base = jax.random.normal(key_base, shape, jnp.float32)
    scale_lo, scale_hi = (0.5, 2.0)
    directions = jax.random.normal(key_dirs, (16, width), jnp.float32)
    coefficients = 0.5 * jax.random.normal(key_coef, (LAYERS, TRAIN, SEQ, 16), jnp.float32)
    token_scale = jnp.exp(jax.random.uniform(key_scale, (LAYERS, TRAIN, SEQ, 1), jnp.float32, jnp.log(scale_lo), jnp.log(scale_hi)))
    rising = 1.0 + 2.0 * jnp.arange(TRAIN, dtype=jnp.float32) / max(TRAIN - 1, 1)
    values = (base + jnp.einsum('ltsk,kw->ltsw', coefficients, directions)) * token_scale * rising[None, :, None, None]
    return jnp.clip(values, -60.0, 60.0).astype(jnp.bfloat16)


def draw_acts(key, part):
    return structured(key, D, 11)


def draw_grads(key, part):
    return structured(key, FF, 23)


def shard_levels(own_key, dims, shards, low, top_value):
    def one(axis_at, parts):
        draws = jax.random.uniform(jax.random.fold_in(jax.random.fold_in(own_key, 6), axis_at), (parts,), jnp.float32, low / len(shards), top_value / len(shards))
        return jnp.repeat(jnp.exp(draws), dims[axis_at] // parts).reshape((-1,) + (1,) * (len(dims) - axis_at - 1))

    loudness = one(*shards[0])
    for cut in shards[1:]:
        loudness = loudness * one(*cut)
    return loudness


def gaussian(rng, extent, spread, bound, cuts=(), held_as=jnp.bfloat16):
    factor_of = shard_levels(rng, extent, cuts, -0.22, 0.18) if cuts else 1.0
    array = jax.random.normal(rng, extent, jnp.float32) * spread * factor_of
    return jnp.minimum(jnp.maximum(array, -bound), bound).astype(held_as)


def setup_inputs(seed: int = 0) -> dict:
    keys = jax.random.split(jax.random.key(seed), 6)
    acts = draw_acts(jax.random.fold_in(keys[5], 71), 0)
    grads = draw_grads(jax.random.fold_in(keys[5], 71), 0)
    proj_in = gaussian(keys[2], (LAYERS, RANK, D), D ** -0.5, 0.09375, ((0, 4),))
    proj_out = gaussian(keys[3], (LAYERS, RANK, FF), FF ** -0.5, 0.046875, ((0, 4),))
    query_grads = gaussian(keys[4], (LAYERS, QUERIES, RANK * RANK), 1.0, 6.0, ((0, 4), (1, 8)))
    return dict(acts=acts, grads=grads, proj_in=proj_in, proj_out=proj_out, query_grads=query_grads)


def precondition(grad, cov_in, cov_out):
    size = cov_in.shape[0]
    identity = jnp.eye(size, dtype=jnp.float32)
    damp_in = 0.1 * jnp.trace(cov_in) / size
    damp_out = 0.1 * jnp.trace(cov_out) / size
    factor_in = jnp.linalg.cholesky(cov_in + damp_in * identity)
    factor_out = jnp.linalg.cholesky(cov_out + damp_out * identity)
    batch, outer, inner = grad.shape
    left_side = grad.transpose(1, 0, 2).reshape(outer, batch * inner)
    left_side = jax.scipy.linalg.cho_solve((factor_out, True), left_side)
    right_side = left_side.reshape(outer, batch, inner).transpose(2, 1, 0).reshape(inner, batch * outer)
    right_side = jax.scipy.linalg.cho_solve((factor_in, True), right_side)
    return right_side.reshape(inner, batch, outer).transpose(1, 2, 0)

def reference(acts, grads, proj_in, proj_out, query_grads):
    highest = lax.Precision.HIGHEST

    def one_layer(layer_items):
        inputs, out_grads, proj_inner, proj_outer, query_rows = layer_items
        proj_acts = jnp.einsum('esd,rd->esr', inputs.astype(jnp.float32), proj_inner.astype(jnp.float32), precision=highest)
        proj_grads = jnp.einsum('esd,rd->esr', out_grads.astype(jnp.float32), proj_outer.astype(jnp.float32), precision=highest)
        tokens = inputs.shape[0] * inputs.shape[1]
        cov_in = jnp.einsum('esr,esq->rq', proj_acts, proj_acts, precision=highest) / tokens
        cov_out = jnp.einsum('esr,esq->rq', proj_grads, proj_grads, precision=highest) / tokens
        grad = jnp.einsum('eso,esi->eoi', proj_grads, proj_acts, precision=highest)
        conditioned = precondition(grad, cov_in, cov_out)
        conditioned = conditioned.reshape(grad.shape[0], -1).astype(jnp.bfloat16)
        return jnp.dot(conditioned.astype(jnp.float32), query_rows.T.astype(jnp.float32), preferred_element_type=jnp.float32)
    per_layer = lax.map(one_layer, (acts, grads, proj_in, proj_out, query_grads))
    summed = lax.optimization_barrier(jnp.sum(per_layer, axis=0))
    return summed / jnp.sqrt(jnp.float32(RANK * RANK * LAYERS * SEQ))
```

```python
import functools
import math

import jax
import jax.numpy as jnp
from jax import lax
from jax.experimental import pallas as pl
from jax.experimental.pallas import tpu as pltpu
from jax.sharding import PartitionSpec as P

HIGHEST = lax.Precision.HIGHEST
ANY = pl.BlockSpec(memory_space=pl.ANY)
VMEM = pl.BlockSpec(memory_space=pltpu.VMEM)
DAMPING = 0.1


def dot(a, b, precision=None):
    return jnp.dot(a, b, precision=precision, preferred_element_type=jnp.float32)


def dot_t(a, b, precision=None):
    return lax.dot_general(
        a, b, (((1,), (1,)), ((), ())), precision=precision, preferred_element_type=jnp.float32
    )


def bits(n):
    return [1 << k for k in range(n.bit_length() - 1)]


def chunk_of(width, limit):
    size = min(width, limit)
    while width % size or size % 128:
        size -= 128
    return size


def project_kernel(chunks, acts, grads, p_in, p_out, cov, grad, a_v, g_v, pi_v, po_v, sems):
    examples, length = a_v.shape[0], a_v.shape[1]
    rank = pi_v.shape[0]
    copies = []
    for src, dst, proj, proj_v, size in (
        (acts, a_v, p_in, pi_v, chunks[0]),
        (grads, g_v, p_out, po_v, chunks[1]),
    ):
        for at in range(0, dst.shape[2], size):
            cut = pl.ds(at, size)
            pair = (
                pltpu.make_async_copy(
                    src.at[0, :, :, cut], dst.at[:, :, cut], sems.at[2 * len(copies)]
                ),
                pltpu.make_async_copy(
                    proj.at[0, :, cut], proj_v.at[:, cut], sems.at[2 * len(copies) + 1]
                ),
            )
            for copy in pair:
                copy.start()
            copies.append((pair, dst, proj_v, at, size))
    sums = [None, None]
    for pair, dst, proj_v, at, size in copies:
        for copy in pair:
            copy.wait()
        rows = dst[:, :, at : at + size].reshape(examples * length, size)
        part = dot_t(proj_v[:, at : at + size], rows)
        k = 0 if dst is a_v else 1
        sums[k] = part if sums[k] is None else sums[k] + part
    both = jnp.concatenate([sums[1], sums[0]], axis=0)
    grams = []
    for e in range(examples):
        cut = both[:, e * length : (e + 1) * length]
        grams.append(dot_t(cut, cut, HIGHEST))
    total = functools.reduce(jnp.add, grams)
    low = lax.broadcasted_iota(jnp.int32, (rank, 2 * rank), 1) < rank
    cov[...] = jnp.where(low, total[:rank], total[rank:])
    for k in range(examples // 2):
        first = pltpu.roll(grams[2 * k][:rank], rank, 1)
        grad[k * rank : (k + 1) * rank, :] = jnp.where(low, first, grams[2 * k + 1][:rank])


def project(acts, grads, p_in, p_out):
    _, examples, length, width = acts.shape
    hidden, rank = grads.shape[3], p_in.shape[1]
    chunks = (chunk_of(width, 4096), chunk_of(hidden, 3584))
    count = 2 * (width // chunks[0] + hidden // chunks[1])
    return pl.pallas_call(
        functools.partial(project_kernel, chunks),
        name="project",
        out_shape=(
            jax.ShapeDtypeStruct((rank, 2 * rank), jnp.float32),
            jax.ShapeDtypeStruct((examples // 2 * rank, 2 * rank), jnp.float32),
        ),
        in_specs=[ANY] * 4,
        out_specs=(VMEM, VMEM),
        scratch_shapes=[
            pltpu.VMEM((examples, length, width), acts.dtype),
            pltpu.VMEM((examples, length, hidden), grads.dtype),
            pltpu.VMEM((rank, width), p_in.dtype),
            pltpu.VMEM((rank, hidden), p_out.dtype),
            pltpu.SemaphoreType.DMA((count,)),
        ],
        cost_estimate=pl.CostEstimate(
            flops=2 * examples * length * rank * (width + hidden),
            bytes_accessed=2 * (examples * length + rank) * (width + hidden),
            transcendentals=0,
        ),
    )(acts, grads, p_in, p_out)


def inverse_plan(rank):
    low = 2 * DAMPING / (rank + 2 * DAMPING)
    scales = []
    while 1 - low > 3e-4:
        prod = low * (2 - low)
        scales.append(2 / (1 + prod))
        low = scales[-1] * prod
    return scales


def inverses(cov):
    rank = cov.shape[0]
    size = 2 * rank
    lane = lax.broadcasted_iota(jnp.int32, (rank, size), 1)
    row = lax.broadcasted_iota(jnp.int32, (rank, size), 0)
    low = lane < rank
    tr_out = jnp.sum(jnp.where(lane == row, cov, 0.0), keepdims=True) / rank
    tr_in = jnp.sum(jnp.where(lane == row + rank, cov, 0.0), keepdims=True) / rank
    big = jnp.concatenate([jnp.where(low, cov, 0.0), jnp.where(low, 0.0, cov)], axis=0)
    eye = (
        lax.broadcasted_iota(jnp.int32, (size, size), 0)
        == lax.broadcasted_iota(jnp.int32, (size, size), 1)
    ).astype(jnp.float32)
    upper = lax.broadcasted_iota(jnp.int32, (size, 1), 0) < rank
    mean = jnp.where(upper, tr_out, tr_in)
    factor = big + (DAMPING * mean) * eye
    start = 2.0 / ((rank + 2 * DAMPING) * mean)
    m = factor * start
    x = None
    scales = inverse_plan(rank)
    for k, c in enumerate(scales):
        q = (2 * c) * eye - c * m
        if x is None:
            x = q
            m = dot(m, q, HIGHEST)
        elif k < len(scales) - 1:
            both = dot(jnp.concatenate([x, m], axis=0), q, HIGHEST)
            x, m = both[:size], both[size:]
        else:
            x = dot(x, q, HIGHEST)
    x = x * start
    rest = eye - dot(factor, x, HIGHEST)
    return x + dot(x, rest, HIGHEST)


def score_kernel(r, tokens, scale, cov_a, cov_b, grad, *refs):
    queries, (out, cond_s, q_v, sems) = refs[:r], refs[r:]
    rank = cov_a.shape[0]
    count = queries[0].shape[0]
    blocks = grad.shape[0] // rank
    mine = lax.rem(lax.axis_index("dp"), r)
    copies = []
    for k in range(r):
        at = pl.multiple_of((mine ^ k) * count, count)
        copy = pltpu.make_async_copy(queries[k], q_v.at[pl.ds(at, count)], sems.at[k])
        copy.start()
        copies.append(copy)
    inv = inverses(cov_a[...] + cov_b[...]) * tokens
    f_out = inv[:rank, :rank]
    f_in = inv[rank:]
    twice_in = jnp.concatenate([pltpu.roll(f_in, rank, 1), f_in], axis=0)
    lined = jnp.concatenate([grad[k * rank : (k + 1) * rank] for k in range(blocks)], axis=1)
    left = dot(f_out, lined, HIGHEST)
    left = jnp.concatenate(
        [left[:, 2 * rank * k : 2 * rank * (k + 1)] for k in range(blocks)], axis=0
    )
    cond = dot(left, twice_in, HIGHEST)
    turned = pltpu.roll(cond, rank, 1)
    n = blocks * rank
    cond_s[0:n, :] = cond
    cond_s[n : 2 * n, :] = turned
    cond_s[2 * n :, :] = cond
    low = lax.broadcasted_iota(jnp.int32, (2 * blocks, 2 * rank), 1) < rank
    parts = []
    for j in range(rank // 2):
        even = cond_s[pl.ds(2 * j, 2 * blocks, stride=rank), :]
        odd = cond_s[pl.ds(n + 2 * j + 1, 2 * blocks, stride=rank), :]
        parts.append(jnp.where(low, even, odd))
    flat = jnp.concatenate(parts, axis=1).astype(jnp.bfloat16)
    for copy in copies:
        copy.wait()
    out[...] = dot_t(flat, q_v[...]) * scale


def scores_of(r, tokens, scale, cov_a, cov_b, grad, queries):
    rank = cov_a.shape[0]
    blocks = grad.shape[0] // rank
    count, width = queries[0].shape
    return pl.pallas_call(
        functools.partial(score_kernel, r, float(tokens), scale),
        name="scores",
        out_shape=jax.ShapeDtypeStruct((2 * blocks, r * count), jnp.float32),
        in_specs=[VMEM] * 3 + [ANY] * r,
        out_specs=VMEM,
        scratch_shapes=[
            pltpu.VMEM((3 * blocks * rank, 2 * rank), jnp.float32),
            pltpu.VMEM((r * count, width), queries[0].dtype),
            pltpu.SemaphoreType.DMA((r,)),
        ],
    )(cov_a, cov_b, grad, *queries)


def local(n_dp, n_layer, acts, grads, proj_in, proj_out, query_grads):
    _, examples, length = acts.shape[:3]
    r = n_dp // n_layer
    assert acts.shape[0] == 1 and examples == 2 and r * n_layer == n_dp

    def swap(x, axis, n, k):
        return lax.ppermute(x, axis, [(i, i ^ k) for i in range(n)])

    queries = [query_grads[0]]
    for k in range(1, r):
        queries.append(swap(query_grads[0], "dp", n_dp, k))
    cov, grad = project(acts, grads, proj_in, proj_out)
    steps = [r * k for k in bits(n_layer)] + bits(r)
    for s, k in enumerate(steps):
        other = swap(cov, "dp", n_dp, k)
        if k >= r:
            grad = jnp.concatenate([grad, swap(grad, "dp", n_dp, k)], axis=0)
        if s < len(steps) - 1:
            cov = cov + other
    width = query_grads.shape[2]
    scale = 1.0 / math.sqrt(width * acts.shape[0] * n_layer * length)
    part = scores_of(r, examples * length * n_dp, scale, cov, other, grad, queries)
    for k in bits(n_layer):
        part = part + swap(part, "layer", n_layer, k)
    pick = (lax.axis_index("dp") // r) ^ lax.axis_index("layer")
    part = lax.dynamic_slice_in_dim(part.reshape(examples, n_layer, -1), pick, 1, axis=1)[:, 0]
    moves = []
    for a in range(n_layer):
        for b in range(r):
            for m in range(n_layer):
                moves.append(((a * r + b) * n_layer + m, (m * r + b) * n_layer + a))
    return lax.ppermute(part, ("dp", "layer"), moves)


def solution(mesh):
    return jax.shard_map(
        functools.partial(local, mesh.shape["dp"], mesh.shape["layer"]),
        mesh=mesh,
        in_specs=(
            P("layer", "dp", None, None),
            P("layer", "dp", None, None),
            P("layer", None, None),
            P("layer", None, None),
            P("layer", "dp", None),
        ),
        out_specs=P("dp", "layer"),
        check_vma=False,
    )
```

```python
import functools
import math

import jax
import jax.numpy as jnp
from jax import lax
from jax.experimental import pallas as pl
from jax.experimental.pallas import tpu as pltpu
from jax.sharding import PartitionSpec as P

HIGHEST = lax.Precision.HIGHEST
ANY = pl.BlockSpec(memory_space=pl.ANY)
VMEM = pl.BlockSpec(memory_space=pltpu.VMEM)
DAMPING = 0.1
PROJECT_VMEM = 16 << 20
SMALL_VMEM = 6 << 20


def dot(a, b, precision=None):
    return jnp.dot(a, b, precision=precision, preferred_element_type=jnp.float32)


def dot_t(a, b, precision=None):
    return lax.dot_general(
        a, b, (((1,), (1,)), ((), ())), precision=precision, preferred_element_type=jnp.float32
    )


def bits(n):
    return [1 << k for k in range(n.bit_length() - 1)]


def chunk_of(width, limit):
    size = min(width, limit)
    while width % size or size % 128:
        size -= 128
    return size


def project_kernel(chunks, acts, grads, p_in, p_out, cov, grad, a_v, g_v, pi_v, po_v, sems):
    examples, length = a_v.shape[0], a_v.shape[1]
    rank = pi_v.shape[0]
    copies = []
    for src, dst, proj, proj_v, size in (
        (acts, a_v, p_in, pi_v, chunks[0]),
        (grads, g_v, p_out, po_v, chunks[1]),
    ):
        for at in range(0, dst.shape[2], size):
            cut = pl.ds(at, size)
            pair = (
                pltpu.make_async_copy(
                    src.at[0, :, :, cut], dst.at[:, :, cut], sems.at[2 * len(copies)]
                ),
                pltpu.make_async_copy(
                    proj.at[0, :, cut], proj_v.at[:, cut], sems.at[2 * len(copies) + 1]
                ),
            )
            for copy in pair:
                copy.start()
            copies.append((pair, dst, proj_v, at, size))
    sums = [None, None]
    for pair, dst, proj_v, at, size in copies:
        for copy in pair:
            copy.wait()
        rows = dst[:, :, at : at + size].reshape(examples * length, size)
        part = dot_t(proj_v[:, at : at + size], rows)
        k = 0 if dst is a_v else 1
        sums[k] = part if sums[k] is None else sums[k] + part
    both = jnp.concatenate([sums[1], sums[0]], axis=0)
    grams = []
    for e in range(examples):
        cut = both[:, e * length : (e + 1) * length]
        grams.append(dot_t(cut, cut, HIGHEST))
    total = functools.reduce(jnp.add, grams)
    low = lax.broadcasted_iota(jnp.int32, (rank, 2 * rank), 1) < rank
    cov[...] = jnp.where(low, total[:rank], total[rank:])
    for k in range(examples // 2):
        first = pltpu.roll(grams[2 * k][:rank], rank, 1)
        grad[k * rank : (k + 1) * rank, :] = jnp.where(low, first, grams[2 * k + 1][:rank])


def project(acts, grads, p_in, p_out):
    _, examples, length, width = acts.shape
    hidden, rank = grads.shape[3], p_in.shape[1]
    chunks = (chunk_of(width, 4096), chunk_of(hidden, 3584))
    count = 2 * (width // chunks[0] + hidden // chunks[1])
    return pl.pallas_call(
        functools.partial(project_kernel, chunks),
        name="project",
        out_shape=(
            jax.ShapeDtypeStruct((rank, 2 * rank), jnp.float32),
            jax.ShapeDtypeStruct((examples // 2 * rank, 2 * rank), jnp.float32),
        ),
        in_specs=[ANY] * 4,
        out_specs=(VMEM, VMEM),
        scratch_shapes=[
            pltpu.VMEM((examples, length, width), acts.dtype),
            pltpu.VMEM((examples, length, hidden), grads.dtype),
            pltpu.VMEM((rank, width), p_in.dtype),
            pltpu.VMEM((rank, hidden), p_out.dtype),
            pltpu.SemaphoreType.DMA((count,)),
        ],
        compiler_params=pltpu.CompilerParams(vmem_limit_bytes=PROJECT_VMEM),
        cost_estimate=pl.CostEstimate(
            flops=2 * examples * length * rank * (width + hidden),
            bytes_accessed=2 * (examples * length + rank) * (width + hidden),
            transcendentals=0,
        ),
    )(*(pltpu.with_memory_space_constraint(x, pltpu.HBM) for x in (acts, grads, p_in, p_out)))


def inverse_plan(rank):
    low = 2 * DAMPING / (rank + 2 * DAMPING)
    scales = []
    while 1 - low > 3e-4:
        prod = low * (2 - low)
        scales.append(2 / (1 + prod))
        low = scales[-1] * prod
    return scales


def inverses(cov):
    rank = cov.shape[0]
    size = 2 * rank
    lane = lax.broadcasted_iota(jnp.int32, (rank, size), 1)
    row = lax.broadcasted_iota(jnp.int32, (rank, size), 0)
    low = lane < rank
    tr_out = jnp.sum(jnp.where(lane == row, cov, 0.0), keepdims=True) / rank
    tr_in = jnp.sum(jnp.where(lane == row + rank, cov, 0.0), keepdims=True) / rank
    big = jnp.concatenate([jnp.where(low, cov, 0.0), jnp.where(low, 0.0, cov)], axis=0)
    eye = (
        lax.broadcasted_iota(jnp.int32, (size, size), 0)
        == lax.broadcasted_iota(jnp.int32, (size, size), 1)
    ).astype(jnp.float32)
    upper = lax.broadcasted_iota(jnp.int32, (size, 1), 0) < rank
    mean = jnp.where(upper, tr_out, tr_in)
    factor = big + (DAMPING * mean) * eye
    start = 2.0 / ((rank + 2 * DAMPING) * mean)
    m = factor * start
    x = None
    scales = inverse_plan(rank)
    for k, c in enumerate(scales):
        q = (2 * c) * eye - c * m
        if x is None:
            x = q
            m = dot(m, q, HIGHEST)
        elif k < len(scales) - 1:
            both = dot(jnp.concatenate([x, m], axis=0), q, HIGHEST)
            x, m = both[:size], both[size:]
        else:
            x = dot(x, q, HIGHEST)
    x = x * start
    rest = eye - dot(factor, x, HIGHEST)
    return x + dot(x, rest, HIGHEST)


def inverse_kernel(tokens, cov_a, cov_b, out):
    out[...] = inverses(cov_a[...] + cov_b[...]) * tokens


def inverses_of(tokens, cov_a, cov_b):
    size = cov_a.shape[1]
    return pl.pallas_call(
        functools.partial(inverse_kernel, float(tokens)),
        name="inverses",
        out_shape=jax.ShapeDtypeStruct((size, size), jnp.float32),
        in_specs=[VMEM] * 2,
        out_specs=VMEM,
        compiler_params=pltpu.CompilerParams(vmem_limit_bytes=SMALL_VMEM),
        cost_estimate=pl.CostEstimate(
            flops=200 * size**3, bytes_accessed=16 * size * size, transcendentals=0
        ),
    )(cov_a, cov_b)


def score_kernel(r, scale, inv, *refs):
    queries, (*grads, out, cond_s, q_v, sems) = refs[:r], refs[r:]
    size = inv.shape[1]
    rank = size // 2
    count = queries[0].shape[0]
    mine = lax.rem(lax.axis_index("dp"), r)
    copies = []
    for k in range(r):
        at = pl.multiple_of((mine ^ k) * count, count)
        copy = pltpu.make_async_copy(queries[k], q_v.at[pl.ds(at, count)], sems.at[k])
        copy.start()
        copies.append(copy)
    f_out = inv[:rank, :rank]
    f_in = inv[rank:, :]
    twice_in = jnp.concatenate([pltpu.roll(f_in, rank, 1), f_in], axis=0)
    pieces = [g[at : at + rank, :] for g in grads for at in range(0, g.shape[0], rank)]
    blocks = len(pieces)
    left = dot(f_out, jnp.concatenate(pieces, axis=1), HIGHEST)
    left = jnp.concatenate([left[:, size * k : size * (k + 1)] for k in range(blocks)], axis=0)
    cond = dot(left, twice_in, HIGHEST)
    n = blocks * rank
    cond_s[0:n, :] = cond
    cond_s[n : 2 * n, :] = pltpu.roll(cond, rank, 1)
    cond_s[2 * n :, :] = cond
    low = lax.broadcasted_iota(jnp.int32, (2 * blocks, size), 1) < rank
    parts = []
    for j in range(rank // 2):
        even = cond_s[pl.ds(2 * j, 2 * blocks, stride=rank), :]
        odd = cond_s[pl.ds(n + 2 * j + 1, 2 * blocks, stride=rank), :]
        parts.append(jnp.where(low, even, odd))
    flat = jnp.concatenate(parts, axis=1).astype(jnp.bfloat16)
    for copy in copies:
        copy.wait()
    out[...] = dot_t(flat, q_v[...]) * scale


def scores_of(r, scale, inv, queries, grads):
    size = inv.shape[1]
    blocks = sum(g.shape[0] for g in grads) // (size // 2)
    count, width = queries[0].shape
    return pl.pallas_call(
        functools.partial(score_kernel, r, scale),
        name="scores",
        out_shape=jax.ShapeDtypeStruct((2 * blocks, r * count), jnp.float32),
        in_specs=[VMEM] + [ANY] * r + [VMEM] * len(grads),
        out_specs=VMEM,
        scratch_shapes=[
            pltpu.VMEM((3 * blocks * (size // 2), size), jnp.float32),
            pltpu.VMEM((r * count, width), queries[0].dtype),
            pltpu.SemaphoreType.DMA((r,)),
        ],
        compiler_params=pltpu.CompilerParams(vmem_limit_bytes=SMALL_VMEM),
        cost_estimate=pl.CostEstimate(
            flops=4 * blocks * r * count * width,
            bytes_accessed=2 * r * count * width,
            transcendentals=0,
        ),
    )(inv, *queries, *grads)


def local(n_dp, n_layer, acts, grads, proj_in, proj_out, query_grads):
    _, examples, length = acts.shape[:3]
    r = n_dp // n_layer
    assert acts.shape[0] == 1 and examples == 2 and r * n_layer == n_dp

    def swap(x, axis, n, k):
        return lax.ppermute(x, axis, [(i, i ^ k) for i in range(n)])

    cov, grad = project(acts, grads, proj_in, proj_out)
    steps = bits(r) + [r * k for k in bits(n_layer)]
    queries = [query_grads[0]]
    for k in range(1, r):
        queries.append(swap(query_grads[0], "dp", n_dp, k))
    gathered = [grad]
    for s, k in enumerate(steps):
        other = swap(cov, "dp", n_dp, k)
        if k >= r:
            whole = jnp.concatenate(gathered, axis=0) if len(gathered) > 1 else gathered[0]
            gathered.append(swap(whole, "dp", n_dp, k))
        if s < len(steps) - 1:
            cov = cov + other
    width = query_grads.shape[2]
    scale = 1.0 / math.sqrt(width * acts.shape[0] * n_layer * length)
    inv = inverses_of(examples * length * n_dp, cov, other)
    part = scores_of(r, scale, inv, queries, gathered)
    for k in bits(n_layer):
        part = part + swap(part, "layer", n_layer, k)
    pick = (lax.axis_index("dp") // r) ^ lax.axis_index("layer")
    part = lax.dynamic_slice_in_dim(part.reshape(examples, n_layer, -1), pick, 1, axis=1)[:, 0]
    moves = []
    for a in range(n_layer):
        for b in range(r):
            for m in range(n_layer):
                moves.append(((a * r + b) * n_layer + m, (m * r + b) * n_layer + a))
    return lax.ppermute(part, ("dp", "layer"), moves)


def solution(mesh):
    n_dp, n_layer = mesh.shape["dp"], mesh.shape["layer"]

    def body(*args):
        return local(n_dp, n_layer, *args)

    return jax.shard_map(
        body,
        mesh=mesh,
        in_specs=(
            P("layer", "dp", None, None),
            P("layer", "dp", None, None),
            P("layer", None, None),
            P("layer", None, None),
            P("layer", "dp", None),
        ),
        out_specs=P("dp", "layer"),
        check_vma=False,
    )
```

```python
import functools
import math

import jax
import jax.numpy as jnp
from jax import lax
from jax.experimental import pallas as pl
from jax.experimental.pallas import tpu as pltpu
from jax.sharding import PartitionSpec as P

HIGHEST = lax.Precision.HIGHEST
ANY = pl.BlockSpec(memory_space=pl.ANY)
VMEM = pl.BlockSpec(memory_space=pltpu.VMEM)
DAMPING = 0.1
PROJECT_VMEM = 16 << 20
SMALL_VMEM = 6 << 20


def dot(a, b, precision=None):
    return jnp.dot(a, b, precision=precision, preferred_element_type=jnp.float32)


def dot_t(a, b, precision=None):
    return lax.dot_general(
        a, b, (((1,), (1,)), ((), ())), precision=precision, preferred_element_type=jnp.float32
    )


def bits(n):
    return [1 << k for k in range(n.bit_length() - 1)]


def chunk_of(width, limit):
    size = min(width, limit)
    while width % size or size % 128:
        size -= 128
    return size


def project_kernel(chunks, depth, acts, grads, p_in, p_out, cov, grad, *scratch):
    a_v, g_v, pi_v, po_v, sums, sems = scratch
    examples, length = a_v.shape[0], a_v.shape[1]
    rank = pi_v.shape[0]
    always = lax.axis_index("dp") >= 0
    loads = []
    for k, (src, dst, proj, proj_v) in enumerate(
        ((acts, a_v, p_in, pi_v), (grads, g_v, p_out, po_v))
    ):
        for at in range(0, dst.shape[2], chunks[k]):
            cut = pl.ds(at, chunks[k])
            sem = 2 * len(loads)
            pair = (
                pltpu.make_async_copy(src.at[0, :, :, cut], dst.at[:, :, cut], sems.at[sem]),
                pltpu.make_async_copy(proj.at[0, :, cut], proj_v.at[:, cut], sems.at[sem + 1]),
            )
            loads.append((pair, k, dst, proj_v, at))

    def start(i):
        if i < len(loads):
            for copy in loads[i][0]:
                copy.start()

    for i in range(depth):
        start(i)
    for i, (pair, k, dst, proj_v, at) in enumerate(loads):
        for copy in pair:
            copy.wait()
        start(i + depth)

        @pl.when(always)
        def _():
            rows = dst[:, :, at : at + chunks[k]].reshape(examples * length, chunks[k])
            part = dot_t(proj_v[:, at : at + chunks[k]], rows)
            sums[k] = part if at == 0 else sums[k] + part

    both = jnp.concatenate([sums[1], sums[0]], axis=0)
    grams = []
    for e in range(examples):
        cut = both[:, e * length : (e + 1) * length]
        grams.append(dot_t(cut, cut, HIGHEST))
    total = functools.reduce(jnp.add, grams)
    low = lax.broadcasted_iota(jnp.int32, (rank, 2 * rank), 1) < rank
    cov[...] = jnp.where(low, total[:rank], total[rank:])
    for k in range(examples // 2):
        first = pltpu.roll(grams[2 * k][:rank], rank, 1)
        grad[k * rank : (k + 1) * rank, :] = jnp.where(low, first, grams[2 * k + 1][:rank])


def project(acts, grads, p_in, p_out):
    _, examples, length, width = acts.shape
    hidden, rank = grads.shape[3], p_in.shape[1]
    chunks = (chunk_of(width, 2048), chunk_of(hidden, 2048))
    count = 2 * (width // chunks[0] + hidden // chunks[1])
    return pl.pallas_call(
        functools.partial(project_kernel, chunks, 4),
        name="project",
        out_shape=(
            jax.ShapeDtypeStruct((rank, 2 * rank), jnp.float32),
            jax.ShapeDtypeStruct((examples // 2 * rank, 2 * rank), jnp.float32),
        ),
        in_specs=[ANY] * 4,
        out_specs=(VMEM, VMEM),
        scratch_shapes=[
            pltpu.VMEM((examples, length, width), acts.dtype),
            pltpu.VMEM((examples, length, hidden), grads.dtype),
            pltpu.VMEM((rank, width), p_in.dtype),
            pltpu.VMEM((rank, hidden), p_out.dtype),
            pltpu.VMEM((2, rank, examples * length), jnp.float32),
            pltpu.SemaphoreType.DMA((count,)),
        ],
        compiler_params=pltpu.CompilerParams(vmem_limit_bytes=PROJECT_VMEM),
        cost_estimate=pl.CostEstimate(
            flops=2 * examples * length * rank * (width + hidden),
            bytes_accessed=2 * (examples * length + rank) * (width + hidden),
            transcendentals=0,
        ),
    )(*(pltpu.with_memory_space_constraint(x, pltpu.HBM) for x in (acts, grads, p_in, p_out)))


def inverse_plan(rank):
    low = 2 * DAMPING / (rank + 2 * DAMPING)
    scales = []
    while 1 - low > 3e-4:
        prod = low * (2 - low)
        scales.append(2 / (1 + prod))
        low = scales[-1] * prod
    return scales


def inverses(cov):
    rank = cov.shape[0]
    size = 2 * rank
    lane = lax.broadcasted_iota(jnp.int32, (rank, size), 1)
    row = lax.broadcasted_iota(jnp.int32, (rank, size), 0)
    low = lane < rank
    tr_out = jnp.sum(jnp.where(lane == row, cov, 0.0), keepdims=True) / rank
    tr_in = jnp.sum(jnp.where(lane == row + rank, cov, 0.0), keepdims=True) / rank
    big = jnp.concatenate([jnp.where(low, cov, 0.0), jnp.where(low, 0.0, cov)], axis=0)
    eye = (
        lax.broadcasted_iota(jnp.int32, (size, size), 0)
        == lax.broadcasted_iota(jnp.int32, (size, size), 1)
    ).astype(jnp.float32)
    upper = lax.broadcasted_iota(jnp.int32, (size, 1), 0) < rank
    mean = jnp.where(upper, tr_out, tr_in)
    factor = big + (DAMPING * mean) * eye
    start = 2.0 / ((rank + 2 * DAMPING) * mean)
    m = factor * start
    x = None
    scales = inverse_plan(rank)
    for k, c in enumerate(scales):
        q = (2 * c) * eye - c * m
        if x is None:
            x = q
            m = dot(m, q, HIGHEST)
        elif k < len(scales) - 1:
            both = dot(jnp.concatenate([x, m], axis=0), q, HIGHEST)
            x, m = both[:size], both[size:]
        else:
            x = dot(x, q, HIGHEST)
    x = x * start
    rest = eye - dot(factor, x, HIGHEST)
    return x + dot(x, rest, HIGHEST)


def inverse_kernel(tokens, cov_a, cov_b, out):
    out[...] = inverses(cov_a[...] + cov_b[...]) * tokens


def inverses_of(tokens, cov_a, cov_b):
    size = cov_a.shape[1]
    return pl.pallas_call(
        functools.partial(inverse_kernel, float(tokens)),
        name="inverses",
        out_shape=jax.ShapeDtypeStruct((size, size), jnp.float32),
        in_specs=[VMEM] * 2,
        out_specs=VMEM,
        compiler_params=pltpu.CompilerParams(vmem_limit_bytes=SMALL_VMEM),
        cost_estimate=pl.CostEstimate(
            flops=200 * size**3, bytes_accessed=16 * size * size, transcendentals=0
        ),
    )(cov_a, cov_b)


def score_kernel(r, scale, inv, *refs):
    queries, (*grads, out, cond_s, q_v, sems) = refs[:r], refs[r:]
    size = inv.shape[1]
    rank = size // 2
    count = queries[0].shape[0]
    mine = lax.rem(lax.axis_index("dp"), r)
    copies = []
    for k in range(r):
        at = pl.multiple_of((mine ^ k) * count, count)
        copy = pltpu.make_async_copy(queries[k], q_v.at[pl.ds(at, count)], sems.at[k])
        copy.start()
        copies.append(copy)
    f_out = inv[:rank, :rank]
    f_in = inv[rank:, :]
    twice_in = jnp.concatenate([pltpu.roll(f_in, rank, 1), f_in], axis=0)
    pieces = [g[at : at + rank, :] for g in grads for at in range(0, g.shape[0], rank)]
    blocks = len(pieces)
    left = dot(f_out, jnp.concatenate(pieces, axis=1), HIGHEST)
    left = jnp.concatenate([left[:, size * k : size * (k + 1)] for k in range(blocks)], axis=0)
    cond = dot(left, twice_in, HIGHEST)
    n = blocks * rank
    cond_s[0:n, :] = cond
    cond_s[n : 2 * n, :] = pltpu.roll(cond, rank, 1)
    cond_s[2 * n :, :] = cond
    low = lax.broadcasted_iota(jnp.int32, (2 * blocks, size), 1) < rank
    parts = []
    for j in range(rank // 2):
        even = cond_s[pl.ds(2 * j, 2 * blocks, stride=rank), :]
        odd = cond_s[pl.ds(n + 2 * j + 1, 2 * blocks, stride=rank), :]
        parts.append(jnp.where(low, even, odd))
    flat = jnp.concatenate(parts, axis=1).astype(jnp.bfloat16)
    for copy in copies:
        copy.wait()
    out[...] = dot_t(flat, q_v[...]) * scale


def scores_of(r, scale, inv, queries, grads):
    size = inv.shape[1]
    blocks = sum(g.shape[0] for g in grads) // (size // 2)
    count, width = queries[0].shape
    return pl.pallas_call(
        functools.partial(score_kernel, r, scale),
        name="scores",
        out_shape=jax.ShapeDtypeStruct((2 * blocks, r * count), jnp.float32),
        in_specs=[VMEM] + [ANY] * r + [VMEM] * len(grads),
        out_specs=VMEM,
        scratch_shapes=[
            pltpu.VMEM((3 * blocks * (size // 2), size), jnp.float32),
            pltpu.VMEM((r * count, width), queries[0].dtype),
            pltpu.SemaphoreType.DMA((r,)),
        ],
        compiler_params=pltpu.CompilerParams(vmem_limit_bytes=SMALL_VMEM),
        cost_estimate=pl.CostEstimate(
            flops=4 * blocks * r * count * width,
            bytes_accessed=2 * r * count * width,
            transcendentals=0,
        ),
    )(inv, *queries, *grads)


def local(n_dp, n_layer, acts, grads, proj_in, proj_out, query_grads):
    _, examples, length = acts.shape[:3]
    r = n_dp // n_layer
    assert acts.shape[0] == 1 and examples == 2 and r * n_layer == n_dp

    def swap(x, axis, n, k):
        return lax.ppermute(x, axis, [(i, i ^ k) for i in range(n)])

    cov, grad = project(acts, grads, proj_in, proj_out)
    steps = bits(r) + [r * k for k in bits(n_layer)]
    queries = [query_grads[0]]
    for k in range(1, r):
        queries.append(swap(query_grads[0], "dp", n_dp, k))
    gathered = [grad]
    for s, k in enumerate(steps):
        other = swap(cov, "dp", n_dp, k)
        if k >= r:
            whole = jnp.concatenate(gathered, axis=0) if len(gathered) > 1 else gathered[0]
            gathered.append(swap(whole, "dp", n_dp, k))
        if s < len(steps) - 1:
            cov = cov + other
    width = query_grads.shape[2]
    scale = 1.0 / math.sqrt(width * acts.shape[0] * n_layer * length)
    inv = inverses_of(examples * length * n_dp, cov, other)
    part = scores_of(r, scale, inv, queries, gathered)
    for k in bits(n_layer):
        part = part + swap(part, "layer", n_layer, k)
    half = n_layer // 2
    pick = (lax.axis_index("dp") // r) ^ lax.axis_index("layer") ^ half
    part = lax.dynamic_slice_in_dim(part.reshape(examples, n_layer, -1), pick, 1, axis=1)[:, 0]
    moves = []
    for a in range(n_layer):
        for b in range(r):
            for m in range(n_layer):
                moves.append(((a * r + b) * n_layer + m, ((m ^ half) * r + b) * n_layer + a))
    return lax.ppermute(part, ("dp", "layer"), moves)


def solution(mesh):
    n_dp, n_layer = mesh.shape["dp"], mesh.shape["layer"]

    def body(*args):
        return local(n_dp, n_layer, *args)

    return jax.shard_map(
        body,
        mesh=mesh,
        in_specs=(
            P("layer", "dp", None, None),
            P("layer", "dp", None, None),
            P("layer", None, None),
            P("layer", None, None),
            P("layer", "dp", None),
        ),
        out_specs=P("dp", "layer"),
        check_vma=False,
    )
```

```python
import functools
import math

import jax
import jax.numpy as jnp
from jax import lax
from jax.experimental import pallas as pl
from jax.experimental.pallas import tpu as pltpu
from jax.sharding import PartitionSpec as P

HIGHEST = lax.Precision.HIGHEST
ANY = pl.BlockSpec(memory_space=pl.ANY)
VMEM = pl.BlockSpec(memory_space=pltpu.VMEM)
DAMPING = 0.1
PROJECT_VMEM = 16 << 20
SMALL_VMEM = 6 << 20


def dot(a, b, precision=None):
    return jnp.dot(a, b, precision=precision, preferred_element_type=jnp.float32)


def dot_t(a, b, precision=None):
    return lax.dot_general(
        a, b, (((1,), (1,)), ((), ())), precision=precision, preferred_element_type=jnp.float32
    )


def bits(n):
    return [1 << k for k in range(n.bit_length() - 1)]


def chunk_of(width, limit):
    size = min(width, limit)
    while width % size or size % 128:
        size -= 128
    return size


def project_kernel(chunks, depth, acts, grads, p_in, p_out, cov, grad, *scratch):
    a_v, g_v, pi_v, po_v, sums, sems = scratch
    examples, length = a_v.shape[0], a_v.shape[1]
    rank = pi_v.shape[0]
    always = lax.axis_index("dp") >= 0
    loads = []
    for k, (src, dst, proj, proj_v) in enumerate(
        ((acts, a_v, p_in, pi_v), (grads, g_v, p_out, po_v))
    ):
        for at in range(0, dst.shape[2], chunks[k]):
            cut = pl.ds(at, chunks[k])
            sem = 2 * len(loads)
            pair = (
                pltpu.make_async_copy(src.at[0, :, :, cut], dst.at[:, :, cut], sems.at[sem]),
                pltpu.make_async_copy(proj.at[0, :, cut], proj_v.at[:, cut], sems.at[sem + 1]),
            )
            loads.append((pair, k, dst, proj_v, at))

    def start(i):
        if i < len(loads):
            for copy in loads[i][0]:
                copy.start()

    for i in range(depth):
        start(i)
    for i, (pair, k, dst, proj_v, at) in enumerate(loads):
        for copy in pair:
            copy.wait()
        start(i + depth)

        @pl.when(always)
        def _():
            rows = dst[:, :, at : at + chunks[k]].reshape(examples * length, chunks[k])
            part = dot_t(proj_v[:, at : at + chunks[k]], rows)
            sums[k] = part if at == 0 else sums[k] + part

    both = jnp.concatenate([sums[1], sums[0]], axis=0)
    grams = []
    for e in range(examples):
        cut = both[:, e * length : (e + 1) * length]
        grams.append(dot_t(cut, cut, HIGHEST))
    total = functools.reduce(jnp.add, grams)
    low = lax.broadcasted_iota(jnp.int32, (rank, 2 * rank), 1) < rank
    cov[...] = jnp.where(low, total[:rank], total[rank:])
    for k in range(examples // 2):
        first = pltpu.roll(grams[2 * k][:rank], rank, 1)
        grad[k * rank : (k + 1) * rank, :] = jnp.where(low, first, grams[2 * k + 1][:rank])


def project(acts, grads, p_in, p_out):
    _, examples, length, width = acts.shape
    hidden, rank = grads.shape[3], p_in.shape[1]
    chunks = (chunk_of(width, 2048), chunk_of(hidden, 2048))
    count = 2 * (width // chunks[0] + hidden // chunks[1])
    return pl.pallas_call(
        functools.partial(project_kernel, chunks, 4),
        name="project",
        out_shape=(
            jax.ShapeDtypeStruct((rank, 2 * rank), jnp.float32),
            jax.ShapeDtypeStruct((examples // 2 * rank, 2 * rank), jnp.float32),
        ),
        in_specs=[ANY] * 4,
        out_specs=(VMEM, VMEM),
        scratch_shapes=[
            pltpu.VMEM((examples, length, width), acts.dtype),
            pltpu.VMEM((examples, length, hidden), grads.dtype),
            pltpu.VMEM((rank, width), p_in.dtype),
            pltpu.VMEM((rank, hidden), p_out.dtype),
            pltpu.VMEM((2, rank, examples * length), jnp.float32),
            pltpu.SemaphoreType.DMA((count,)),
        ],
        compiler_params=pltpu.CompilerParams(vmem_limit_bytes=PROJECT_VMEM),
        cost_estimate=pl.CostEstimate(
            flops=2 * examples * length * rank * (width + hidden),
            bytes_accessed=2 * (examples * length + rank) * (width + hidden),
            transcendentals=0,
        ),
    )(*(pltpu.with_memory_space_constraint(x, pltpu.HBM) for x in (acts, grads, p_in, p_out)))


def inverse_plan(rank):
    low = 2 * DAMPING / (rank + 2 * DAMPING)
    scales = []
    while 1 - low > 3e-4:
        prod = low * (2 - low)
        scales.append(2 / (1 + prod))
        low = scales[-1] * prod
    return scales


def inverses(cov):
    rank = cov.shape[0]
    size = 2 * rank
    lane = lax.broadcasted_iota(jnp.int32, (rank, size), 1)
    row = lax.broadcasted_iota(jnp.int32, (rank, size), 0)
    low = lane < rank
    tr_out = jnp.sum(jnp.where(lane == row, cov, 0.0), keepdims=True) / rank
    tr_in = jnp.sum(jnp.where(lane == row + rank, cov, 0.0), keepdims=True) / rank
    big = jnp.concatenate([jnp.where(low, cov, 0.0), jnp.where(low, 0.0, cov)], axis=0)
    eye = (
        lax.broadcasted_iota(jnp.int32, (size, size), 0)
        == lax.broadcasted_iota(jnp.int32, (size, size), 1)
    ).astype(jnp.float32)
    upper = lax.broadcasted_iota(jnp.int32, (size, 1), 0) < rank
    mean = jnp.where(upper, tr_out, tr_in)
    factor = big + (DAMPING * mean) * eye
    start = 2.0 / ((rank + 2 * DAMPING) * mean)
    m = factor * start
    x = None
    scales = inverse_plan(rank)
    for k, c in enumerate(scales):
        q = (2 * c) * eye - c * m
        if x is None:
            x = q
            m = dot(m, q, HIGHEST)
        elif k < len(scales) - 1:
            both = dot(jnp.concatenate([x, m], axis=0), q, HIGHEST)
            x, m = both[:size], both[size:]
        else:
            x = dot(x, q, HIGHEST)
    x = x * start
    rest = eye - dot(factor, x, HIGHEST)
    return x + dot(x, rest, HIGHEST)


def inverse_kernel(tokens, cov_a, cov_b, out):
    out[...] = inverses(cov_a[...] + cov_b[...]) * tokens


def inverses_of(tokens, cov_a, cov_b):
    size = cov_a.shape[1]
    return pl.pallas_call(
        functools.partial(inverse_kernel, float(tokens)),
        name="inverses",
        out_shape=jax.ShapeDtypeStruct((size, size), jnp.float32),
        in_specs=[VMEM] * 2,
        out_specs=VMEM,
        compiler_params=pltpu.CompilerParams(vmem_limit_bytes=SMALL_VMEM),
        cost_estimate=pl.CostEstimate(
            flops=200 * size**3, bytes_accessed=16 * size * size, transcendentals=0
        ),
    )(cov_a, cov_b)


def score_kernel(r, order, scale, inv, *refs):
    queries, (*grads, out, cond_s) = refs[:r], refs[r:]
    size = inv.shape[1]
    rank = size // 2
    count = queries[0].shape[0]
    f_out = inv[:rank, :rank]
    f_in = inv[rank:, :]
    twice_in = jnp.concatenate([pltpu.roll(f_in, rank, 1), f_in], axis=0)
    came = [(g, at) for g in grads for at in range(0, g.shape[0], rank)]
    blocks = len(came)
    pieces = [g[at : at + rank, :] for g, at in (came[order.index(k)] for k in range(blocks))]
    left = dot(f_out, jnp.concatenate(pieces, axis=1), HIGHEST)
    left = jnp.concatenate([left[:, size * k : size * (k + 1)] for k in range(blocks)], axis=0)
    cond = dot(left, twice_in, HIGHEST)
    n = blocks * rank
    cond_s[0:n, :] = cond
    cond_s[n : 2 * n, :] = pltpu.roll(cond, rank, 1)
    cond_s[2 * n :, :] = cond
    low = lax.broadcasted_iota(jnp.int32, (2 * blocks, size), 1) < rank
    parts = []
    for j in range(rank // 2):
        even = cond_s[pl.ds(2 * j, 2 * blocks, stride=rank), :]
        odd = cond_s[pl.ds(n + 2 * j + 1, 2 * blocks, stride=rank), :]
        parts.append(jnp.where(low, even, odd))
    flat = jnp.concatenate(parts, axis=1).astype(jnp.bfloat16)
    held = jnp.concatenate([q[...] for q in queries], axis=0)
    scores = dot_t(flat, held) * scale
    mine = lax.rem(lax.axis_index("dp"), r)
    for k in bits(r):
        turned = jnp.concatenate(
            [scores[:, (c ^ k) * count : ((c ^ k) + 1) * count] for c in range(r)], axis=1
        )
        scores = jnp.where((mine & k) != 0, turned, scores)
    out[...] = scores


def scores_of(r, order, scale, inv, queries, grads):
    size = inv.shape[1]
    blocks = sum(g.shape[0] for g in grads) // (size // 2)
    count, width = queries[0].shape
    return pl.pallas_call(
        functools.partial(score_kernel, r, order, scale),
        name="scores",
        out_shape=jax.ShapeDtypeStruct((2 * blocks, r * count), jnp.float32),
        in_specs=[VMEM] * (1 + r + len(grads)),
        out_specs=VMEM,
        scratch_shapes=[pltpu.VMEM((3 * blocks * (size // 2), size), jnp.float32)],
        compiler_params=pltpu.CompilerParams(vmem_limit_bytes=SMALL_VMEM),
        cost_estimate=pl.CostEstimate(
            flops=4 * blocks * r * count * width,
            bytes_accessed=2 * r * count * width,
            transcendentals=0,
        ),
    )(inv, *queries, *grads)


def local(n_dp, n_layer, acts, grads, proj_in, proj_out, query_grads):
    _, examples, length = acts.shape[:3]
    r = n_dp // n_layer
    assert acts.shape[0] == 1 and examples == 2 and r * n_layer == n_dp

    def swap(x, axis, n, k):
        return lax.ppermute(x, axis, [(i, i ^ k) for i in range(n)])

    cov, grad = project(acts, grads, proj_in, proj_out)
    steps = bits(r) + [r * k for k in reversed(bits(n_layer))]
    queries = [query_grads[0]]
    for k in range(1, r):
        queries.append(swap(query_grads[0], "dp", n_dp, k))
    gathered, order = [grad], [0]
    for s, k in enumerate(steps):
        other = swap(cov, "dp", n_dp, k)
        if k >= r:
            whole = jnp.concatenate(gathered, axis=0) if len(gathered) > 1 else gathered[0]
            gathered.append(swap(whole, "dp", n_dp, k))
            order += [o ^ (k // r) for o in order]
        if s < len(steps) - 1:
            cov = cov + other
    width = query_grads.shape[2]
    scale = 1.0 / math.sqrt(width * acts.shape[0] * n_layer * length)
    inv = inverses_of(examples * length * n_dp, cov, other)
    part = scores_of(r, order, scale, inv, queries, gathered)
    for k in bits(n_layer):
        part = part + swap(part, "layer", n_layer, k)
    half = n_layer // 2
    pick = (lax.axis_index("dp") // r) ^ lax.axis_index("layer") ^ half
    part = lax.dynamic_slice_in_dim(part.reshape(examples, n_layer, -1), pick, 1, axis=1)[:, 0]
    moves = []
    for a in range(n_layer):
        for b in range(r):
            for m in range(n_layer):
                moves.append(((a * r + b) * n_layer + m, ((m ^ half) * r + b) * n_layer + a))
    return lax.ppermute(part, ("dp", "layer"), moves)


def solution(mesh):
    n_dp, n_layer = mesh.shape["dp"], mesh.shape["layer"]

    def body(*args):
        return local(n_dp, n_layer, *args)

    return jax.shard_map(
        body,
        mesh=mesh,
        in_specs=(
            P("layer", "dp", None, None),
            P("layer", "dp", None, None),
            P("layer", None, None),
            P("layer", None, None),
            P("layer", "dp", None),
        ),
        out_specs=P("dp", "layer"),
        check_vma=False,
    )
```
